512 devices in a mesh: dp: 16 (over z_lo, x), ctx: 32 (over y, z_hi, core).
Axes of the slice: x: 4, y: 4, z: 16 (z_hi: 4, z_lo: 4; z = z_hi * 4 + z_lo), core: 2. Of those that a mesh axis runs over, the one named last changes fastest.
Arguments:
- tokens: bfloat16 [16, 4096, 4096], P('dp', 'ctx'), may hold values from -6 to 6
- grad_attn: bfloat16 [16, 4096, 1024], P('dp', 'ctx'), may hold values from -6 to 6
- w_packed: bfloat16 [10240, 128], P('ctx'), may hold values from -0.1875 to 0.1875
- block_rows: int32 [10, 8], replicated, may hold values from 0 to 31, as said below
- span_pairs: int32 [32, 2], replicated, may hold values from 0 to 63, as said below
Outputs:
- grad_tokens: bfloat16 [16, 4096, 4096], P('dp', 'ctx')
- grad_weights: float32 [10240, 128], P('ctx')
The draws below stay inside these ranges and needn't reach their ends.
Inputs may be any that keep to these rules, and one draw needn't show every extreme that they name: `block_rows`: row c lists the 8 row blocks in which column block c is nonzero, all different; rows 0 to 3 together list each of the 32 row blocks exactly once. Index k of ctx holds spans span_pairs[k, 0] and span_pairs[k, 1] = 63 - span_pairs[k, 0]; the first column takes each of 0 to 31 once.
All inputs are finite; a program needn't handle non-finite values.
Results may differ from the reference program's by a relative error of at most 0.0087.
Values may be sent and summed in bfloat16 or wider, within the bound.
A program may use at most 64 MiB of HBM per device.

```python
import math
import jax
import jax.numpy as jnp
from jax import lax

D = 4096
HD = 128
BLK = 128
QPG = 8
GROUPS = 1
SPAN = 64
NRB = 32
NBR = 8
NCB = 10
NNZ = 80
TOK_DEV = 128
SEQ = 4096
SEQS = 16
N_CTX = 32


def draw_block_rows(key, part):
    first_cover = jax.random.permutation(jax.random.fold_in(key, 11), NRB)
    cover = NRB // NBR
    columns = []
    for column in range(NCB):
        if column < cover:
            columns.append(first_cover[column * NBR:(column + 1) * NBR])
        else:
            columns.append(jax.random.permutation(jax.random.fold_in(key, 100 + column), NRB)[:NBR])
    return jnp.stack(columns).astype(jnp.int32)


def draw_span_pairs(key, part):
    span_order = jax.random.permutation(jax.random.fold_in(key, 7), N_CTX).astype(jnp.int32)
    return jnp.stack([span_order, 2 * N_CTX - 1 - span_order], axis=1).astype(jnp.int32)


def level_of(key, extent, cuts, smallest, top_value):
    level = 1.0
    for axis_at, shards_of in cuts:
        draws = jax.random.uniform(jax.random.fold_in(jax.random.fold_in(key, 6), axis_at), (shards_of,), jnp.float32, smallest / len(cuts), top_value / len(cuts))
        level = level * jnp.repeat(jnp.exp(draws), extent[axis_at] // shards_of).reshape((-1,) + (1,) * (len(extent) - 1 - axis_at))
    return level


def normal_values(key, extent, scale, limit, split=(), kind=jnp.bfloat16):
    drawn = scale * jax.random.normal(key, extent, jnp.float32)
    if split:
        drawn = drawn * level_of(key, extent, split, -0.22, 0.18)
    return jnp.clip(drawn, -limit, limit).astype(kind)


def setup_inputs(seed: int = 0) -> dict:
    key_of = jax.random.split(jax.random.key(seed), 6)
    tokens = normal_values(key_of[0], (SEQS, SEQ, D), 1.0, 6.0, ((0, 16), (1, 32)))
    grad_attn = normal_values(key_of[1], (SEQS, SEQ, GROUPS * QPG * HD), 1.0, 6.0, ((0, 16), (1, 32)))
    w_packed = normal_values(key_of[2], (NNZ * BLK, BLK), (NBR * BLK) ** -0.5, 0.1875, ((0, 32),))
    block_rows = draw_block_rows(jax.random.fold_in(key_of[5], 71), 0)
    span_pairs = draw_span_pairs(jax.random.fold_in(key_of[5], 71), 0)
    return {"tokens": tokens, "grad_attn": grad_attn, "w_packed": w_packed, "block_rows": block_rows, "span_pairs": span_pairs}


EPSILON = 1e-06
HIGH = lax.Precision.HIGHEST

def norm_forward(values):
    factor = lax.rsqrt(lax.optimization_barrier(jnp.mean(values * values, axis=-1, keepdims=True)) + EPSILON)
    return (values * factor, factor)

def norm_backward(values, factor, upstream):
    return factor * upstream - values * (factor * factor * factor) * lax.optimization_barrier(jnp.mean(upstream * values, axis=-1, keepdims=True))

def reference(tokens, grad_attn, w_packed, block_rows, span_pairs):
    nquery = GROUPS * QPG
    score_scale = 1.0 / math.sqrt(HD)
    weights = w_packed.reshape(NCB, NBR, BLK, BLK).astype(jnp.float32)
    flat_ids = block_rows.reshape(-1)
    onehot = (flat_ids[:, None] == jnp.arange(NRB, dtype=jnp.int32)[None, :]).astype(jnp.float32)
    positions = (span_pairs[:, :, None] * SPAN + jnp.arange(SPAN, dtype=jnp.int32)[None, None, :]).reshape(-1).astype(jnp.int32)
    length = positions.shape[0]
    nblocks = length // TOK_DEV

    def one_sequence(running, inputs):
        token_rows, upstream_rows = inputs
        selected = jnp.take(token_rows.reshape(length, NRB, BLK), flat_ids, axis=1).reshape(length, NCB, NBR, BLK)
        projected = jnp.einsum('tcri,crio->tco', selected.astype(jnp.float32), weights, precision=HIGH).astype(jnp.bfloat16)
        query_raw = projected[:, :nquery].astype(jnp.float32).reshape(length, GROUPS, QPG, HD)
        key_raw = projected[:, nquery:nquery + GROUPS].astype(jnp.float32)
        values = projected[:, nquery + GROUPS:].astype(jnp.float32)
        query_norm, query_factor = norm_forward(query_raw)
        key_norm, key_factor = norm_forward(key_raw)
        query_hat = query_norm.astype(jnp.bfloat16).astype(jnp.float32)
        key_hat = key_norm.astype(jnp.bfloat16).astype(jnp.float32)
        upstream = upstream_rows.reshape(length, GROUPS, QPG, HD).astype(jnp.float32)

        def scores_of(first_row):
            query_block = lax.dynamic_slice_in_dim(query_hat, first_row, TOK_DEV, 0)
            query_pos = lax.dynamic_slice_in_dim(positions, first_row, TOK_DEV, 0)
            raw_scores = jnp.einsum('tgqd,ugd->tgqu', query_block, key_hat, precision=HIGH) * score_scale
            keep = positions[None, None, None, :] <= query_pos[:, None, None, None]
            return (query_block, jnp.where(keep, jnp.exp(raw_scores), 0.0))

        def forward_block(block_index):
            first_row = block_index * TOK_DEV
            query_block, exp_scores = scores_of(first_row)
            totals = lax.optimization_barrier(jnp.sum(exp_scores, axis=-1))
            expo_low = lax.optimization_barrier(exp_scores.astype(jnp.bfloat16)).astype(jnp.float32)
            attn = jnp.einsum('tgqu,ugd->tgqd', expo_low, values, precision=HIGH) / totals[..., None]
            grad_rows = lax.dynamic_slice_in_dim(upstream, first_row, TOK_DEV, 0)
            return (totals, lax.optimization_barrier(jnp.sum(grad_rows * attn, axis=-1)))
        totals_all, deltas_all = lax.map(forward_block, jnp.arange(nblocks, dtype=jnp.int32))

        def backward_block(sums, block_index):
            key_sum, value_sum = sums
            first_row = block_index * TOK_DEV
            query_block, exp_scores = scores_of(first_row)
            prob = exp_scores / totals_all[block_index][..., None]
            prob_low = lax.optimization_barrier(prob.astype(jnp.bfloat16)).astype(jnp.float32)
            grad_rows = lax.dynamic_slice_in_dim(upstream, first_row, TOK_DEV, 0)
            dprob = jnp.einsum('tgqd,ugd->tgqu', grad_rows, values, precision=HIGH)
            dscore = (prob * (dprob - deltas_all[block_index][..., None]) * score_scale).astype(jnp.bfloat16)
            dscore = lax.optimization_barrier(dscore).astype(jnp.float32)
            grad_query_block = jnp.einsum('tgqu,ugd->tgqd', dscore, key_hat, precision=HIGH)
            key_sum = key_sum + jnp.einsum('tgqu,tgqd->ugd', dscore, query_block, precision=HIGH)
            value_sum = value_sum + jnp.einsum('tgqu,tgqd->ugd', prob_low, grad_rows, precision=HIGH)
            return ((key_sum, value_sum), grad_query_block)
        empty_kv = jnp.zeros((length, GROUPS, HD), jnp.float32)
        (grad_key_hat, grad_value), grad_query_blocks = lax.scan(backward_block, (empty_kv, empty_kv), jnp.arange(nblocks, dtype=jnp.int32))
        grad_query_hat = grad_query_blocks.reshape(length, GROUPS, QPG, HD)
        grad_query = norm_backward(query_raw, query_factor, grad_query_hat).astype(jnp.bfloat16)
        grad_key = norm_backward(key_raw, key_factor, grad_key_hat).astype(jnp.bfloat16)
        grad_proj = jnp.concatenate([grad_query.reshape(length, nquery, HD), grad_key, grad_value.astype(jnp.bfloat16)], axis=1)
        grad_proj_wide = grad_proj.astype(jnp.float32)
        spread = jnp.einsum('tco,crio->tcri', grad_proj_wide, weights, precision=HIGH).reshape(length, NNZ, BLK)
        grad_rows_out = jnp.einsum('tki,kb->tbi', spread, onehot, precision=HIGH).reshape(length, D).astype(jnp.bfloat16)
        device_sel = selected.reshape(nblocks, TOK_DEV, NCB, NBR, BLK)
        device_grad = grad_proj.reshape(nblocks, TOK_DEV, NCB, HD)

        def add_partial(total, pieces):
            token_part, grad_part = pieces
            partial_w = jnp.einsum('tcri,tco->crio', token_part.astype(jnp.float32), grad_part.astype(jnp.float32), precision=HIGH).astype(jnp.bfloat16)
            partial_w = lax.optimization_barrier(partial_w)
            return (total + partial_w.astype(jnp.float32), None)
        running, unused = lax.scan(add_partial, running, (device_sel, device_grad))
        return (running, grad_rows_out)
    start_sum = jnp.zeros((NCB, NBR, BLK, BLK), jnp.float32)
    grad_w, grad_x = lax.scan(one_sequence, start_sum, (tokens, grad_attn))
    return (grad_x, grad_w.reshape(NNZ * BLK, BLK))
```

```python
import functools
import math

import jax
import jax.numpy as jnp
from jax import lax
from jax.experimental import pallas as pl
from jax.experimental.pallas import tpu as pltpu
from jax.sharding import PartitionSpec as P

D = 4096
HD = 128
BLK = 128
QPG = 8
SPAN = 64
NRB = 32
NBR = 8
NCB = 10
EPSILON = 1e-06
SCALE = 1.0 / math.sqrt(HD)
SHARD = 320
PIECE = 80
CHUNK = 256
BF = jnp.bfloat16
F32 = jnp.float32
MESH = pl.DeviceIdType.MESH


def place():
    dp = lax.axis_index("dp")
    ctx = lax.axis_index("ctx")
    return dp % 4, dp // 4, ctx // 8, (ctx // 2) % 4, ctx % 2


def peers():
    x, l, y, h, c = place()

    def at(px, plo, py, ph, pc):
        return (plo * 4 + px, py * 8 + ph * 2 + pc)

    return {
        "x": lambda d: at((x + d) % 4, l, y, h, c),
        "l": lambda d: at(x, (l + d) % 4, y, h, c),
        "y": lambda d: at(x, l, (y + d) % 4, h, c),
        "h": lambda d: at(x, l, y, (h + d) % 4, c),
        "c": lambda d: at(x, l, y, h, (c + d) % 2),
    }


def remote(src, dst, send, recv, device):
    return pltpu.make_async_remote_copy(
        src_ref=src, dst_ref=dst, send_sem=send, recv_sem=recv, device_id=device, device_id_type=MESH
    )


def enter(targets):
    barrier = pltpu.get_barrier_semaphore()
    for target in targets:
        pl.semaphore_signal(barrier, inc=1, device_id=target, device_id_type=MESH)
    pl.semaphore_wait(barrier, len(targets))


def rsqrt_mean(values):
    return lax.rsqrt(jnp.mean(values * values, axis=-1, keepdims=True) + EPSILON)


def forward_kernel(
    tok_ref, w_ref, rows_ref, kv_out, w_out, proj_ref, tokt_ref,
    tokb, wb, wall, kvb, loc, outs,
    wzs, wzr, wys, wyr, wxs, wxr, wcs, wcr, kzs, kzr, kys, kyr, kcs, kcr,
):
    x, l, y, h, c = place()
    to = peers()
    enter([to[a](d) for a in ("h", "y", "x") for d in (1, 2, 3)] + [to["c"](1)])
    sent = []

    def go(copy):
        copy.start()
        sent.append(copy)

    def w_x(d, yy):
        return remote(
            wb.at[c, x, yy], wb.at[c, x, yy], wxs.at[d - 1, yy], wxr.at[d - 1, yy], to["x"](d)
        )

    def w_c(xx, yy):
        piece = wb.at[c, xx, yy]
        return remote(piece, piece, wcs.at[xx, yy], wcr.at[xx, yy], to["c"](1))

    own = w_ref.at[pl.ds(pl.multiple_of(x * PIECE, 16), PIECE)]
    mine = pltpu.make_async_copy(own, wb.at[c, x, y, h], loc.at[0])
    mine.start()
    zs = [
        remote(own, wb.at[c, x, y, h], wzs.at[d - 1], wzr.at[d - 1], to["h"](d)) for d in (2, 1, 3)
    ]
    for copy in zs:
        go(copy)
    for b in range(NRB):
        tokb[b] = tok_ref[:, b * BLK : (b + 1) * BLK]
        tokt_ref[b] = tok_ref[:, b * BLK : (b + 1) * BLK].T
    mine.wait()
    for copy in zs:
        copy.wait_recv()
    ys = [
        remote(wb.at[c, x, y], wb.at[c, x, y], wys.at[d - 1], wyr.at[d - 1], to["y"](d))
        for d in (2, 1, 3)
    ]
    for copy in ys:
        go(copy)
    for yy in (3, 0, 1, 2):

        @pl.when(y != yy)
        def _():
            back = (y + 3 - yy) % 4
            remote(
                wb.at[c, x, yy], wb.at[c, x, yy], wys.at[back], wyr.at[back], to["y"](1)
            ).wait_recv()

        for d in (2, 1, 3):
            go(w_x(d, yy))
        go(w_c(x, yy))

    def forward_x(yy):
        for d in (1, 3, 2):
            w_x(d, yy).wait_recv()
            go(w_c((x + 4 - d) % 4, yy))

    def assemble(yy):
        for xx in range(4):
            w_c(xx, yy).wait_recv()
        for cc in range(2):
            for hh in range(4):
                for q in range(4):
                    row = ((yy * 4 + hh) * 2 + cc) * SHARD + q * PIECE
                    wall[row : row + PIECE, :] = wb[cc, q, yy, hh]

    def project(col):
        chosen = jnp.concatenate(
            [tokb[rows_ref[col, r]] for r in range(NBR)], axis=1
        )
        rows = NBR * BLK
        return jnp.dot(
            chosen, wall[col * rows : (col + 1) * rows, :], preferred_element_type=F32
        ).astype(BF)

    forward_x(3)
    assemble(3)
    key = project(QPG)
    value = project(QPG + 1)
    proj_ref[QPG] = key
    proj_ref[QPG + 1] = value
    wide = key.astype(F32)
    kvb[c, y, h, 0:128, :] = (wide * rsqrt_mean(wide)).astype(BF)
    kvb[c, y, h, 128:256, :] = value

    def k_y(d, hh):
        piece = kvb.at[c, y, hh]
        return remote(piece, piece, kys.at[d - 1, hh], kyr.at[d - 1, hh], to["y"](d))

    def k_c(yy, hh):
        piece = kvb.at[c, yy, hh]
        return remote(piece, piece, kcs.at[yy, hh], kcr.at[yy, hh], to["c"](1))

    kz = [
        remote(kvb.at[c, y, h], kvb.at[c, y, h], kzs.at[d - 1], kzr.at[d - 1], to["h"](d))
        for d in (1, 2, 3)
    ]
    for d in (2, 1, 3):
        go(kz[d - 1])
    for d in (2, 1, 3):
        go(k_y(d, h))
    go(k_c(y, h))
    for yy in (0, 1, 2):
        forward_x(yy)
    for d in (1, 3, 2):
        kz[d - 1].wait_recv()
        hh = (h + 4 - d) % 4
        for e in (2, 1, 3):
            go(k_y(e, hh))
        go(k_c(y, hh))
    for yy in (0, 1, 2):
        assemble(yy)
    save_w = pltpu.make_async_copy(wall, w_out, loc.at[1])
    save_w.start()
    for col in range(QPG):
        proj_ref[col] = project(col)
    for step in (0, 1, 3, 2):
        hh = (h + 4 - step) % 4
        for d in (1, 3, 2):
            k_y(d, hh).wait_recv()
            go(k_c((y + 4 - d) % 4, hh))
    saves = []
    for step in (0, 1, 3, 2):
        hh = (h + 4 - step) % 4
        for yy in range(4):
            k_c(yy, hh).wait_recv()
    for cc in range(2):
        save = pltpu.make_async_copy(kvb.at[cc], kv_out.at[cc], outs.at[cc])
        save.start()
        saves.append(save)
    for copy in sent:
        copy.wait_send()
    for save in saves:
        save.wait()
    save_w.wait()


def attention_kernel(
    pairs_ref, kv_ref, proj_ref, up_ref, gp_ref, dkv_ref,
    ks, vs, kt, vt, es, dk, dv, qh, qt, gg, gt, dd, acc, tot,
):
    me = lax.axis_index("ctx")

    def gather(owner, _):
        spot = (owner % 2) * 16 + owner // 2
        for part in range(2):
            at = pl.multiple_of(pairs_ref[owner, part] * SPAN, SPAN)
            ks[pl.ds(at, SPAN), :] = kv_ref[spot, part * SPAN : (part + 1) * SPAN, :]
            vs[pl.ds(at, SPAN), :] = kv_ref[spot, 128 + part * SPAN : 128 + (part + 1) * SPAN, :]
        return 0

    lax.fori_loop(0, 32, gather, 0)

    def chunks(part):
        return ((pairs_ref[me, part] + 1) * SPAN + CHUNK - 1) // CHUNK

    def rows_of(index):
        return pl.ds(pl.multiple_of(index * CHUNK, CHUNK), CHUNK)

    def flip(index, _):
        kt[index] = ks[rows_of(index), :].T
        vt[index] = vs[rows_of(index), :].T
        return 0

    lax.fori_loop(0, chunks(1), flip, 0)

    def part_rows(part, head):
        return slice(head * SPAN, (head + 1) * SPAN), slice(part * SPAN, (part + 1) * SPAN)

    for part in range(2):
        for head in range(QPG):
            put, get = part_rows(part, head)
            raw = proj_ref[head, get, :].astype(F32)
            qh[part, put, :] = (raw * rsqrt_mean(raw)).astype(BF)
            gg[part, put, :] = up_ref[get, head * HD : (head + 1) * HD]
        qt[part] = qh[part].T

    factor = SCALE * math.log2(math.e)

    def forward(part):
        count = chunks(part)
        acc[...] = jnp.zeros_like(acc)
        tot[...] = jnp.zeros_like(tot)

        def tile(index, masked):
            score = jnp.dot(ks[rows_of(index), :], qt[part], preferred_element_type=F32)
            expo = jnp.exp2(score * factor)
            if masked:
                key_pos = index * CHUNK + lax.broadcasted_iota(jnp.int32, expo.shape, 0)
                query_pos = pairs_ref[me, part] * SPAN + lax.broadcasted_iota(
                    jnp.int32, expo.shape, 1
                ) % SPAN
                expo = jnp.where(key_pos <= query_pos, expo, 0.0)
            tot[...] += jnp.sum(expo.reshape(CHUNK // 8, 8, expo.shape[1]), axis=0)
            low = expo.astype(BF)
            es[part * 8 + index] = low
            acc[...] += jnp.dot(vt[index], low, preferred_element_type=F32)

        def step(index, _):
            tile(index, False)
            return 0

        lax.fori_loop(0, count - 1, step, 0)
        tile(count - 1, True)
        inverse = 1.0 / jnp.sum(tot[...], axis=0, keepdims=True)
        up = gg[part].astype(F32).T
        delta = jnp.sum(up * (acc[...] * inverse), axis=0, keepdims=True)
        scaled = inverse * SCALE
        low = (up * scaled).astype(BF)
        gt[part] = low
        gg[part] = low.T
        dd[part] = jnp.broadcast_to(delta * scaled, dd.shape[1:])

    def backward(part, first):
        count = chunks(part)
        acc[...] = jnp.zeros_like(acc)

        def step(index, _):
            low = es[part * 8 + index]
            dprob = jnp.dot(vs[rows_of(index), :], gt[part], preferred_element_type=F32)
            dscore = (low.astype(F32) * (dprob - dd[part, 0:1, :])).astype(BF)
            more_k = jnp.dot(dscore, qh[part], preferred_element_type=F32)
            more_v = jnp.dot(low, gg[part], preferred_element_type=F32)
            if first:
                dk[rows_of(index), :] = more_k
                dv[rows_of(index), :] = more_v
            else:
                dk[rows_of(index), :] += more_k
                dv[rows_of(index), :] += more_v
            acc[...] += jnp.dot(kt[index], dscore, preferred_element_type=F32)
            return 0

        lax.fori_loop(0, count, step, 0)
        grad = acc[...].T
        for head in range(QPG):
            put, get = part_rows(part, head)
            up = grad[put, :]
            raw = proj_ref[head, get, :].astype(F32)
            rq = rsqrt_mean(raw)
            gp_ref[head, get, :] = (
                rq * up - raw * (rq * rq * rq) * jnp.mean(up * raw, axis=-1, keepdims=True)
            ).astype(BF)

    forward(1)
    forward(0)
    backward(1, True)
    backward(0, False)

    def clear(index, _):
        dk[rows_of(index), :] = jnp.zeros((CHUNK, HD), F32)
        dv[rows_of(index), :] = jnp.zeros((CHUNK, HD), F32)
        return 0

    lax.fori_loop(chunks(1), 4096 // CHUNK, clear, 0)

    def scatter(owner, _):
        spot = (owner % 2) * 16 + owner // 2
        for part in range(2):
            at = pl.multiple_of(pairs_ref[owner, part] * SPAN, SPAN)
            low = part * SPAN
            dkv_ref[spot, low : low + SPAN, :] = dk[pl.ds(at, SPAN), :].astype(BF)
            dkv_ref[spot, 128 + low : 128 + low + SPAN, :] = (
                dv[pl.ds(at, SPAN), :] * math.sqrt(HD)
            ).astype(BF)
        return 0

    lax.fori_loop(0, 32, scatter, 0)


def reduce_kernel(
    dkv_ref, gpq_ref, proj_ref, tokt_ref, rows_ref, gw_ref, gpkv_ref,
    rc, sb, ry, s2, rz, pw, wc, sx, rx, ty, wy, tz, wz, tl, rl, og,
    dcs, dcr, dys, dyr, dzs, dzr, pcs, pcr, pxs, pxr, pys, pyr, pzs, pzr, pls, plr, pgs, pgr,
):
    x, l, y, h, c = place()
    to = peers()
    enter([to[a](d) for a in ("h", "y", "x", "l") for d in (1, 2, 3)] + [to["c"](1)])
    sent = []

    def go(copy):
        copy.start()
        sent.append(copy)

    def d_c(yy):
        return remote(dkv_ref.at[1 - c, yy], rc.at[yy], dcs.at[yy], dcr.at[yy], to["c"](1))

    for d in (2, 1, 3, 0):
        go(d_c((y + d) % 4))

    def partial(col, grad):
        chosen = jnp.concatenate([tokt_ref[rows_ref[col, r]] for r in range(NBR)], axis=0)
        rows = NBR * BLK
        pw[col * rows : (col + 1) * rows, :] = jnp.dot(
            chosen, grad, preferred_element_type=F32
        ).astype(BF)

    def d_y(d, hh):
        return remote(
            sb.at[(y + d) % 4, hh], ry.at[d - 1, hh], dys.at[d - 1, hh], dyr.at[d - 1, hh], to["y"](d)
        )

    for d in (2, 1, 3, 0):
        yy = (y + d) % 4
        d_c(yy).wait_recv()
        for step in (2, 1, 3, 0):
            hh = (h + step) % 4
            sb[yy, hh] = (dkv_ref[c, yy, hh].astype(F32) + rc[yy, hh].astype(F32)).astype(BF)
            if d:
                go(d_y(d, hh))

    def p_c(yy, hh):
        row = ((yy * 4 + hh) * 2 + 1 - c) * SHARD
        return remote(
            pw.at[pl.ds(pl.multiple_of(row, 64), SHARD)],
            wc.at[yy, hh],
            pcs.at[yy, hh],
            pcr.at[yy, hh],
            to["c"](1),
        )

    for col in range(QPG):
        partial(col, gpq_ref[col])
    for yy in (0, 1, 2):
        for hh in range(4):
            go(p_c(yy, hh))

    d_z = [
        remote(s2.at[(h + d) % 4], rz.at[d - 1], dzs.at[d - 1], dzr.at[d - 1], to["h"](d))
        for d in (1, 2, 3)
    ]
    for step in (2, 1, 3, 0):
        hh = (h + step) % 4
        total = sb[y, hh].astype(F32)
        for d in (1, 3, 2):
            d_y(d, hh).wait_recv()
            total = total + ry[d - 1, hh].astype(F32)
        s2[hh] = total.astype(BF)
        if step:
            go(d_z[step - 1])

    def p_x(d, yy):
        return remote(
            sx.at[(x + d) % 4, yy], rx.at[d - 1, yy], pxs.at[d - 1, yy], pxr.at[d - 1, yy], to["x"](d)
        )

    def fold_core(yy):
        for hh in range(4):
            p_c(yy, hh).wait_recv()
            row = pl.multiple_of(((yy * 4 + hh) * 2 + c) * SHARD, 64)
            for q in range(4):
                sx[q, yy, hh] = (
                    pw[pl.ds(row + q * PIECE, PIECE), :].astype(F32)
                    + wc[yy, hh, q * PIECE : (q + 1) * PIECE, :].astype(F32)
                ).astype(BF)
        for d in (2, 1, 3):
            go(p_x(d, yy))

    def p_y(yy):
        d = (yy + 3 - y) % 4
        return remote(ty.at[yy], wy.at[d], pys.at[yy], pyr.at[d], (l * 4 + x, yy * 8 + h * 2 + c))

    def fold_x(yy):
        total = sx[x, yy].astype(F32)
        for d in (1, 3, 2):
            p_x(d, yy).wait_recv()
            total = total + rx[d - 1, yy].astype(F32)
        ty[yy] = total.astype(BF)

        @pl.when(y != yy)
        def _():
            p_y(yy).start()

    p_z = [
        remote(tz.at[(h + d) % 4], wz.at[d - 1], pzs.at[d - 1], pzr.at[d - 1], to["h"](d))
        for d in (1, 2, 3)
    ]
    p_l = [
        remote(tl, rl.at[d - 1], pls.at[d - 1], plr.at[d - 1], to["l"](d)) for d in (1, 2, 3)
    ]
    p_g = [
        remote(og.at[x], og.at[x], pgs.at[d - 1], pgr.at[d - 1], to["x"](d)) for d in (1, 2, 3)
    ]

    def finish():
        total = ty[y].astype(F32)
        for d in (1, 3, 2):
            remote(ty.at[0], wy.at[d - 1], pys.at[0], pyr.at[d - 1], to["y"](1)).wait_recv()
            total = total + wy[d - 1].astype(F32)
        tz[...] = total.astype(BF)
        for d in (2, 1, 3):
            p_z[d - 1].start()
        total = tz[h].astype(F32)
        for d in (1, 3, 2):
            p_z[d - 1].wait_recv()
            total = total + wz[d - 1].astype(F32)
        tl[...] = total
        for d in (2, 1, 3):
            p_l[d - 1].start()
        for d in (1, 3, 2):
            p_l[d - 1].wait_recv()
            total = total + rl[d - 1]
        og[x] = total
        for d in (2, 1, 3):
            p_g[d - 1].start()

    for yy in (0, 1, 2):
        fold_core(yy)
    total = s2[h].astype(F32)
    for d in (1, 3, 2):
        d_z[d - 1].wait_recv()
        total = total + rz[d - 1].astype(F32)
    up = total[0:128]
    raw = proj_ref[QPG].astype(F32)
    rk = rsqrt_mean(raw)
    grad_key = (
        rk * up - raw * (rk * rk * rk) * jnp.mean(up * raw, axis=-1, keepdims=True)
    ).astype(BF)
    grad_value = total[128:256].astype(BF)
    gpkv_ref[0] = grad_key
    gpkv_ref[1] = grad_value
    partial(QPG, grad_key)
    partial(QPG + 1, grad_value)
    for hh in range(4):
        go(p_c(3, hh))
    for yy in (0, 1, 2):
        fold_x(yy)
    fold_core(3)
    fold_x(3)
    finish()
    for copy in p_g:
        copy.wait_recv()
    for q in range(4):
        gw_ref[q * PIECE : (q + 1) * PIECE, :] = og[q]
    for copy in sent + p_z + p_l + p_g:
        copy.wait_send()
    for yy in range(4):

        @pl.when(y != yy)
        def _():
            p_y(yy).wait_send()


def tokens_kernel(gpq_ref, gpkv_ref, w_ref, rows_ref, out_ref, acc):
    rows = NBR * BLK
    for col in range(NCB):
        grad = gpq_ref[col] if col < QPG else gpkv_ref[col - QPG]
        spread = lax.dot_general(
            grad,
            w_ref[col * rows : (col + 1) * rows, :],
            (((1,), (1,)), ((), ())),
            preferred_element_type=F32,
        )
        for r in range(NBR):
            at = pl.ds(pl.multiple_of(rows_ref[col, r] * BLK, BLK), BLK)
            piece = spread[:, r * BLK : (r + 1) * BLK]
            if col < NRB // NBR:
                acc[:, at] = piece
            else:
                acc[:, at] += piece
    out_ref[...] = acc[...].astype(BF)


VM = pl.BlockSpec(memory_space=pltpu.VMEM)
SM = pl.BlockSpec(memory_space=pltpu.SMEM)
HB = pl.BlockSpec(memory_space=pl.ANY)
LIMIT = 60 * 1024 * 1024


def dma(*shape):
    return pltpu.SemaphoreType.DMA(shape)


def shape(dims, kind=BF):
    return jax.ShapeDtypeStruct(dims, kind)


def run_forward(tokens, w, block_rows):
    return pl.pallas_call(
        forward_kernel,
        out_shape=(
            shape((2, 4, 4, 256, HD)),
            shape((NCB * NBR * BLK, BLK)),
            shape((NCB, 128, HD)),
            shape((NRB, BLK, 128)),
        ),
        in_specs=[VM, VM, SM],
        out_specs=(HB, HB, VM, VM),
        scratch_shapes=[
            pltpu.VMEM((NRB, 128, BLK), BF),
            pltpu.VMEM((2, 4, 4, 4, PIECE, BLK), BF),
            pltpu.VMEM((NCB * NBR * BLK, BLK), BF),
            pltpu.VMEM((2, 4, 4, 256, HD), BF),
            dma(2), dma(2),
            dma(3), dma(3), dma(3), dma(3), dma(3, 4), dma(3, 4), dma(4, 4), dma(4, 4),
            dma(3), dma(3), dma(3, 4), dma(3, 4), dma(4, 4), dma(4, 4),
        ],
        compiler_params=pltpu.CompilerParams(
            collective_id=0, has_side_effects=True, vmem_limit_bytes=LIMIT
        ),
        name="forward",
    )(tokens, w, block_rows)


def run_attention(pairs, kv, proj, upstream):
    rows = QPG * SPAN
    return pl.pallas_call(
        attention_kernel,
        out_shape=(shape((QPG, 128, HD)), shape((32, 256, HD))),
        in_specs=[SM, VM, VM, VM],
        out_specs=(VM, VM),
        scratch_shapes=[
            pltpu.VMEM((4096, HD), BF),
            pltpu.VMEM((4096, HD), BF),
            pltpu.VMEM((16, HD, CHUNK), BF),
            pltpu.VMEM((16, HD, CHUNK), BF),
            pltpu.VMEM((24, CHUNK, rows), BF),
            pltpu.VMEM((4096, HD), F32),
            pltpu.VMEM((4096, HD), F32),
            pltpu.VMEM((2, rows, HD), BF),
            pltpu.VMEM((2, HD, rows), BF),
            pltpu.VMEM((2, rows, HD), BF),
            pltpu.VMEM((2, HD, rows), BF),
            pltpu.VMEM((2, 8, rows), F32),
            pltpu.VMEM((HD, rows), F32),
            pltpu.VMEM((8, rows), F32),
        ],
        compiler_params=pltpu.CompilerParams(vmem_limit_bytes=LIMIT),
        name="attention",
    )(pairs, kv, proj, upstream)


def run_reduce(dkv, gpq, proj, tokt, block_rows):
    return pl.pallas_call(
        reduce_kernel,
        out_shape=(shape((SHARD, BLK), F32), shape((2, 128, HD))),
        in_specs=[VM, VM, VM, VM, SM],
        out_specs=(VM, VM),
        scratch_shapes=[
            pltpu.VMEM((4, 4, 256, HD), BF),
            pltpu.VMEM((4, 4, 256, HD), BF),
            pltpu.VMEM((3, 4, 256, HD), BF),
            pltpu.VMEM((4, 256, HD), BF),
            pltpu.VMEM((3, 256, HD), BF),
            pltpu.VMEM((NCB * NBR * BLK, BLK), BF),
            pltpu.VMEM((4, 4, SHARD, BLK), BF),
            pltpu.VMEM((4, 4, 4, PIECE, BLK), BF),
            pltpu.VMEM((3, 4, 4, PIECE, BLK), BF),
            pltpu.VMEM((4, 4, PIECE, BLK), BF),
            pltpu.VMEM((3, 4, PIECE, BLK), BF),
            pltpu.VMEM((4, PIECE, BLK), BF),
            pltpu.VMEM((3, PIECE, BLK), BF),
            pltpu.VMEM((PIECE, BLK), F32),
            pltpu.VMEM((3, PIECE, BLK), F32),
            pltpu.VMEM((4, PIECE, BLK), F32),
            dma(4), dma(4), dma(3, 4), dma(3, 4), dma(3), dma(3),
            dma(4, 4), dma(4, 4), dma(3, 4), dma(3, 4), dma(4), dma(3),
            dma(3), dma(3), dma(3), dma(3), dma(3), dma(3),
        ],
        compiler_params=pltpu.CompilerParams(
            collective_id=1, has_side_effects=True, vmem_limit_bytes=LIMIT
        ),
        name="reduce",
    )(dkv, gpq, proj, tokt, block_rows)


def run_tokens(gpq, gpkv, w_all, block_rows):
    return pl.pallas_call(
        tokens_kernel,
        out_shape=shape((128, D)),
        in_specs=[VM, VM, VM, SM],
        out_specs=VM,
        scratch_shapes=[pltpu.VMEM((128, D), F32)],
        compiler_params=pltpu.CompilerParams(vmem_limit_bytes=LIMIT),
        name="tokens",
    )(gpq, gpkv, w_all, block_rows)


def per_device(tokens, grad_attn, w_packed, block_rows, span_pairs):
    kv, w_all, proj, tokt = run_forward(tokens[0], w_packed, block_rows)
    gpq, dkv = run_attention(span_pairs, kv.reshape(32, 256, HD), proj, grad_attn[0])
    grad_weights, gpkv = run_reduce(dkv.reshape(2, 4, 4, 256, HD), gpq, proj, tokt, block_rows)
    grad_tokens = run_tokens(gpq, gpkv, w_all, block_rows)
    return (grad_tokens[None], grad_weights)


def solution(mesh):
    in_specs = (P("dp", "ctx", None), P("dp", "ctx", None), P("ctx", None), P(), P())
    out_specs = (P("dp", "ctx", None), P("ctx", None))
    return jax.shard_map(
        per_device, mesh=mesh, in_specs=in_specs, out_specs=out_specs, check_vma=False
    )
```

```python
import functools
import math

import jax
import jax.numpy as jnp
from jax import lax
from jax.experimental import pallas as pl
from jax.experimental.pallas import tpu as pltpu
from jax.sharding import PartitionSpec as P

D = 4096
HD = 128
BLK = 128
QPG = 8
SPAN = 64
NRB = 32
NBR = 8
NCB = 10
EPSILON = 1e-06
SCALE = 1.0 / math.sqrt(HD)
SHARD = 320
PIECE = 80
CHUNK = 512
BF = jnp.bfloat16
F32 = jnp.float32
MESH = pl.DeviceIdType.MESH


def place():
    dp = lax.axis_index("dp")
    ctx = lax.axis_index("ctx")
    return dp % 4, dp // 4, ctx // 8, (ctx // 2) % 4, ctx % 2


def peers():
    x, l, y, h, c = place()

    def at(px, plo, py, ph, pc):
        return (plo * 4 + px, py * 8 + ph * 2 + pc)

    return {
        "x": lambda d: at((x + d) % 4, l, y, h, c),
        "l": lambda d: at(x, (l + d) % 4, y, h, c),
        "y": lambda d: at(x, l, (y + d) % 4, h, c),
        "h": lambda d: at(x, l, y, (h + d) % 4, c),
        "c": lambda d: at(x, l, y, h, (c + d) % 2),
    }


def remote(src, dst, send, recv, device):
    return pltpu.make_async_remote_copy(
        src_ref=src, dst_ref=dst, send_sem=send, recv_sem=recv, device_id=device, device_id_type=MESH
    )


def enter(targets):
    barrier = pltpu.get_barrier_semaphore()
    for target in targets:
        pl.semaphore_signal(barrier, inc=1, device_id=target, device_id_type=MESH)
    pl.semaphore_wait(barrier, len(targets))


class Ring:
    def __init__(self, own, at, send, recv):
        to = peers()
        h = place()[3]
        up, down = to["h"](1), to["h"](3)
        self.own = [
            remote(own(0), at(h, 0), send.at[0], recv.at[0], up),
            remote(own(1), at(h, 1), send.at[1], recv.at[1], down),
            remote(own(1), at(h, 1), send.at[2], recv.at[2], up),
            remote(own(0), at(h, 0), send.at[3], recv.at[3], down),
        ]
        before, after = at((h + 3) % 4, 0), at((h + 1) % 4, 1)
        self.relay = [
            remote(before, before, send.at[4], recv.at[4], up),
            remote(after, after, send.at[5], recv.at[5], down),
        ]


class RingSum:
    def __init__(self, terms, relayed, landed, halves, send, recv):
        to = peers()
        self.h = place()[3]
        up, down = to["h"](1), to["h"](3)
        self.terms, self.relayed, self.landed, self.halves = terms, relayed, landed, halves
        h, (a, b) = self.h, halves
        far, nxt, prev = (h + 2) % 4, (h + 1) % 4, (h + 3) % 4
        self.first = [
            remote(terms.at[far, a], relayed.at[a], send.at[0], recv.at[0], up),
            remote(terms.at[far, b], relayed.at[b], send.at[1], recv.at[1], down),
        ]
        self.direct = [
            remote(terms.at[nxt, b], landed.at[0, b], send.at[2], recv.at[2], up),
            remote(terms.at[prev, a], landed.at[1, a], send.at[3], recv.at[3], down),
        ]
        self.added = [
            remote(terms.at[nxt, a], landed.at[0, a], send.at[4], recv.at[4], up),
            remote(terms.at[prev, b], landed.at[1, b], send.at[5], recv.at[5], down),
        ]

    def pass_on(self, go):
        h, (a, b) = self.h, self.halves
        for index, half, target in ((0, a, (h + 1) % 4), (1, b, (h + 3) % 4)):
            self.first[index].wait_recv()
            self.terms[target, half] = (
                self.terms[target, half].astype(F32) + self.relayed[half].astype(F32)
            ).astype(BF)
            go(self.added[index])

    def result(self):
        for copy in self.direct + self.added:
            copy.wait_recv()
        return (
            self.terms[self.h].astype(F32)
            + self.landed[0].astype(F32)
            + self.landed[1].astype(F32)
        )


def rsqrt_mean(values):
    return lax.rsqrt(jnp.mean(values * values, axis=-1, keepdims=True) + EPSILON)


def forward_kernel(
    tok_ref, w_ref, table_ref, kv_out, w_out, proj_ref, tokt_ref,
    rows_ref, tokb, wb, wall, kvb, loc, outs,
    wzs, wzr, wys, wyr, wxs, wxr, wcs, wcr, kzs, kzr, kys, kyr, kcs, kcr,
):
    x, l, y, h, c = place()
    to = peers()
    table = pltpu.make_async_copy(table_ref, rows_ref, loc.at[2])
    table.start()
    enter(
        [to[a](d) for a in ("y", "x") for d in (1, 2, 3)] + [to["h"](1), to["h"](3), to["c"](1)]
    )
    sent = []

    def go(copy):
        copy.start()
        sent.append(copy)

    def w_x(d, yy):
        return remote(
            wb.at[c, x, yy], wb.at[c, x, yy], wxs.at[d - 1, yy], wxr.at[d - 1, yy], to["x"](d)
        )

    def w_c(xx, yy):
        piece = wb.at[c, xx, yy]
        return remote(piece, piece, wcs.at[xx, yy], wcr.at[xx, yy], to["c"](1))

    row = pl.multiple_of(x * PIECE, 16)
    mine = pltpu.make_async_copy(w_ref.at[pl.ds(row, PIECE)], wb.at[c, x, y, h], loc.at[0])
    mine.start()
    w_cut = ((0, 48), (48, 32))
    wz = Ring(
        lambda half: w_ref.at[pl.ds(row + w_cut[half][0], w_cut[half][1])],
        lambda hh, half: wb.at[c, x, y, hh, pl.ds(*w_cut[half])],
        wzs,
        wzr,
    )
    for copy in wz.own:
        go(copy)
    for b in range(NRB):
        tokb[b] = tok_ref[:, b * BLK : (b + 1) * BLK]
        tokt_ref[b] = tok_ref[:, b * BLK : (b + 1) * BLK].T
    mine.wait()
    for index in range(2):
        wz.own[index].wait_recv()
        go(wz.relay[index])
    for copy in wz.own[2:] + wz.relay:
        copy.wait_recv()
    ys = [
        remote(wb.at[c, x, y], wb.at[c, x, y], wys.at[d - 1], wyr.at[d - 1], to["y"](d))
        for d in (2, 1, 3)
    ]
    sent.extend(ys)

    @pl.when(y == 3)
    def _():
        for copy in ys:
            copy.start()

    for yy in (3, 0, 1, 2):

        @pl.when(y != yy)
        def _():
            back = (y + 3 - yy) % 4
            remote(
                wb.at[c, x, yy], wb.at[c, x, yy], wys.at[back], wyr.at[back], to["y"](1)
            ).wait_recv()

        for d in (2, 1, 3):
            go(w_x(d, yy))
        go(w_c(x, yy))
        if yy == 3:

            @pl.when(y != 3)
            def _():
                for copy in ys:
                    copy.start()

    def forward_x(yy):
        for d in (1, 3, 2):
            w_x(d, yy).wait_recv()
            go(w_c((x + 4 - d) % 4, yy))

    def assemble(yy):
        for xx in range(4):
            w_c(xx, yy).wait_recv()
        for cc in range(2):
            for hh in range(4):
                for q in range(4):
                    row = ((yy * 4 + hh) * 2 + cc) * SHARD + q * PIECE
                    wall[row : row + PIECE, :] = wb[cc, q, yy, hh]

    def project(col):
        chosen = jnp.concatenate(
            [tokb[rows_ref[r, col]] for r in range(NBR)], axis=1
        )
        rows = NBR * BLK
        return jnp.dot(
            chosen, wall[col * rows : (col + 1) * rows, :], preferred_element_type=F32
        ).astype(BF)

    forward_x(3)
    table.wait()
    assemble(3)
    key = project(QPG)
    value = project(QPG + 1)
    proj_ref[QPG] = key
    proj_ref[QPG + 1] = value
    wide = key.astype(F32)
    kvb[c, y, h, 0:128, :] = (wide * rsqrt_mean(wide)).astype(BF)
    kvb[c, y, h, 128:256, :] = value

    def k_y(d, hh):
        piece = kvb.at[c, y, hh]
        return remote(piece, piece, kys.at[d - 1, hh], kyr.at[d - 1, hh], to["y"](d))

    def k_c(yy, hh):
        piece = kvb.at[c, yy, hh]
        return remote(piece, piece, kcs.at[yy, hh], kcr.at[yy, hh], to["c"](1))

    k_cut = ((0, 128), (128, 128))
    kz = Ring(
        lambda half: kvb.at[c, y, h, pl.ds(*k_cut[half])],
        lambda hh, half: kvb.at[c, y, hh, pl.ds(*k_cut[half])],
        kzs,
        kzr,
    )
    for copy in kz.own:
        go(copy)
    for d in (2, 1, 3):
        go(k_y(d, h))
    go(k_c(y, h))
    for yy in (0, 1, 2):
        forward_x(yy)
    for index in range(2):
        kz.own[index].wait_recv()
        go(kz.relay[index])
    for d in (1, 3, 2):
        for copy in {1: (kz.own[2],), 3: (kz.own[3],), 2: kz.relay}[d]:
            copy.wait_recv()
        hh = (h + 4 - d) % 4
        for e in (2, 1, 3):
            go(k_y(e, hh))
        go(k_c(y, hh))
    for yy in (0, 1, 2):
        assemble(yy)
    save_w = pltpu.make_async_copy(wall, w_out, loc.at[1])
    save_w.start()
    for col in range(QPG):
        proj_ref[col] = project(col)
    for step in (0, 1, 3, 2):
        hh = (h + 4 - step) % 4
        for d in (1, 3, 2):
            k_y(d, hh).wait_recv()
            go(k_c((y + 4 - d) % 4, hh))
    saves = []
    for step in (0, 1, 3, 2):
        hh = (h + 4 - step) % 4
        for yy in range(4):
            k_c(yy, hh).wait_recv()
        for cc in range(2):
            save = pltpu.make_async_copy(kvb.at[cc, :, hh], kv_out.at[cc, :, hh], outs.at[cc, step])
            save.start()
            saves.append(save)
    for copy in sent:
        copy.wait_send()
    for save in saves:
        save.wait()
    save_w.wait()


def attention_kernel(
    table_ref, kv_ref, proj_ref, up_ref, gp_ref, dkv_ref,
    pairs_ref, sems, ks, vs, kt, vt, es, dk, dv, qh, qt, gg, gt, dd, acc, tot,
):
    me = lax.axis_index("ctx")

    table = pltpu.make_async_copy(table_ref, pairs_ref, sems.at[0])
    table.start()

    def gather(owner, _):
        spot = (owner % 2) * 16 + owner // 2
        for part in range(2):
            at = pl.ds(pl.multiple_of(pairs_ref[part, owner] * SPAN, SPAN), SPAN)
            for half, into in ((0, ks), (1, vs)):
                pltpu.make_async_copy(
                    kv_ref.at[spot, pl.ds(half * 128 + part * SPAN, SPAN)],
                    into.at[at],
                    sems.at[1 + half],
                ).start()
        return 0

    def chunks(part):
        return ((pairs_ref[part, me] + 1) * SPAN + CHUNK - 1) // CHUNK

    def rows_of(index):
        return pl.ds(pl.multiple_of(index * CHUNK, CHUNK), CHUNK)

    def flip(index, _):
        kt[index] = ks[rows_of(index), :].T
        vt[index] = vs[rows_of(index), :].T
        return 0

    def part_rows(part, head):
        return slice(head * SPAN, (head + 1) * SPAN), slice(part * SPAN, (part + 1) * SPAN)

    table.wait()
    lax.fori_loop(0, 32, gather, 0)
    for part in range(2):
        for head in range(QPG):
            put, get = part_rows(part, head)
            raw = proj_ref[head, get, :].astype(F32)
            qh[part, put, :] = (raw * rsqrt_mean(raw)).astype(BF)
            gg[part, put, :] = up_ref[get, head * HD : (head + 1) * HD]
        qt[part] = qh[part].T

    pltpu.make_async_copy(ks, ks, sems.at[1]).wait()
    pltpu.make_async_copy(vs, vs, sems.at[2]).wait()
    lax.fori_loop(0, chunks(1), flip, 0)
    factor = SCALE * math.log2(math.e)

    def forward(part):
        count = chunks(part)
        acc[...] = jnp.zeros_like(acc)
        tot[...] = jnp.zeros_like(tot)

        def tile(index, masked):
            score = jnp.dot(ks[rows_of(index), :], qt[part], preferred_element_type=F32)
            expo = jnp.exp2(score * factor)
            if masked:
                key_pos = index * CHUNK + lax.broadcasted_iota(jnp.int32, expo.shape, 0)
                query_pos = pairs_ref[part, me] * SPAN + lax.broadcasted_iota(
                    jnp.int32, expo.shape, 1
                ) % SPAN
                expo = jnp.where(key_pos <= query_pos, expo, 0.0)
            tot[...] += jnp.sum(expo.reshape(CHUNK // 8, 8, expo.shape[1]), axis=0)
            low = expo.astype(BF)
            es[part * (2048 // CHUNK) + index] = low
            acc[...] += jnp.dot(vt[index], low, preferred_element_type=F32)

        def step(index, _):
            tile(index, False)
            return 0

        lax.fori_loop(0, count - 1, step, 0)
        tile(count - 1, True)
        inverse = 1.0 / jnp.sum(tot[...], axis=0, keepdims=True)
        up = gg[part].astype(F32).T
        delta = jnp.sum(up * (acc[...] * inverse), axis=0, keepdims=True)
        scaled = inverse * SCALE
        low = (up * scaled).astype(BF)
        gt[part] = low
        gg[part] = low.T
        dd[part] = jnp.broadcast_to(delta * scaled, dd.shape[1:])

    def backward(part, first):
        count = chunks(part)
        acc[...] = jnp.zeros_like(acc)

        def step(index, _):
            low = es[part * (2048 // CHUNK) + index]
            dprob = jnp.dot(vs[rows_of(index), :], gt[part], preferred_element_type=F32)
            dscore = (low.astype(F32) * (dprob - dd[part, 0:1, :])).astype(BF)
            more_k = jnp.dot(dscore, qh[part], preferred_element_type=F32)
            more_v = jnp.dot(low, gg[part], preferred_element_type=F32)
            if first:
                dk[rows_of(index), :] = more_k
                dv[rows_of(index), :] = more_v
            else:
                dk[rows_of(index), :] += more_k
                dv[rows_of(index), :] += more_v
            acc[...] += jnp.dot(kt[index], dscore, preferred_element_type=F32)
            return 0

        lax.fori_loop(0, count, step, 0)
        grad = acc[...].T
        for head in range(QPG):
            put, get = part_rows(part, head)
            up = grad[put, :]
            raw = proj_ref[head, get, :].astype(F32)
            rq = rsqrt_mean(raw)
            gp_ref[head, get, :] = (
                rq * up - raw * (rq * rq * rq) * jnp.mean(up * raw, axis=-1, keepdims=True)
            ).astype(BF)

    forward(1)
    forward(0)
    backward(1, True)
    backward(0, False)

    def clear(index, _):
        dk[rows_of(index), :] = jnp.zeros((CHUNK, HD), F32)
        dv[rows_of(index), :] = jnp.zeros((CHUNK, HD), F32)
        return 0

    lax.fori_loop(chunks(1), 4096 // CHUNK, clear, 0)

    def scatter(owner, _):
        spot = (owner % 2) * 16 + owner // 2
        for part in range(2):
            at = pl.multiple_of(pairs_ref[part, owner] * SPAN, SPAN)
            low = part * SPAN
            dkv_ref[spot, low : low + SPAN, :] = dk[pl.ds(at, SPAN), :].astype(BF)
            dkv_ref[spot, 128 + low : 128 + low + SPAN, :] = (
                dv[pl.ds(at, SPAN), :] * math.sqrt(HD)
            ).astype(BF)
        return 0

    lax.fori_loop(0, 32, scatter, 0)


def reduce_kernel(
    dkv_ref, gpq_ref, proj_ref, tokens_ref, table_ref, gw_ref, gpkv_ref,
    rows_ref, tokt_ref, dl, loc, rc, sb, ry, s2, rf, rz, pw, wc, sx, rx, ty, wy, tz, wf, wz, lb, og,
    dcs, dcr, dys, dyr, dzs, dzr, pcs, pcr, pxs, pxr, pys, pyr, pzs, pzr, pls, plr, pgs, pgr,
):
    x, l, y, h, c = place()
    to = peers()
    table = pltpu.make_async_copy(table_ref, rows_ref, loc.at[4])
    turned = pltpu.make_async_copy(tokens_ref, tokt_ref, loc.at[5])
    loads = [pltpu.make_async_copy(dkv_ref.at[c, yy], dl.at[yy], loc.at[yy]) for yy in range(4)]
    for copy in loads + [table, turned]:
        copy.start()
    enter(
        [to[a](d) for a in ("y", "x", "l") for d in (1, 2, 3)]
        + [to["h"](1), to["h"](3), to["c"](1)]
    )
    sent = []

    def go(copy):
        copy.start()
        sent.append(copy)

    def d_c(yy):
        return remote(dkv_ref.at[1 - c, yy], rc.at[yy], dcs.at[yy], dcr.at[yy], to["c"](1))

    for d in (2, 1, 3, 0):
        go(d_c((y + d) % 4))

    def partial(col, grad):
        chosen = jnp.concatenate([tokt_ref[rows_ref[r, col]] for r in range(NBR)], axis=0)
        rows = NBR * BLK
        pw[col * rows : (col + 1) * rows, :] = jnp.dot(
            chosen, grad, preferred_element_type=F32
        ).astype(BF)

    def d_y(d, hh):
        return remote(
            sb.at[(y + d) % 4, hh], ry.at[d - 1, hh], dys.at[d - 1, hh], dyr.at[d - 1, hh], to["y"](d)
        )

    for copy in loads:
        copy.wait()
    for d in (2, 1, 3, 0):
        yy = (y + d) % 4
        d_c(yy).wait_recv()
        for step in (2, 1, 3, 0):
            hh = (h + step) % 4
            sb[yy, hh] = (dl[yy, hh].astype(F32) + rc[yy, hh].astype(F32)).astype(BF)
            if d:
                go(d_y(d, hh))

    def p_c(yy, hh):
        row = ((yy * 4 + hh) * 2 + 1 - c) * SHARD
        return remote(
            pw.at[pl.ds(pl.multiple_of(row, 64), SHARD)],
            wc.at[yy, hh],
            pcs.at[yy, hh],
            pcr.at[yy, hh],
            to["c"](1),
        )

    table.wait()
    turned.wait()
    for col in range(QPG):
        partial(col, gpq_ref[col])
    for yy in (0, 1, 2):
        for hh in range(4):
            go(p_c(yy, hh))

    d_z = RingSum(s2, rf, rz, (slice(0, 128), slice(128, 256)), dzs, dzr)
    for step in (2, 1, 3, 0):
        hh = (h + step) % 4
        total = sb[y, hh].astype(F32)
        for d in (1, 3, 2):
            d_y(d, hh).wait_recv()
            total = total + ry[d - 1, hh].astype(F32)
        s2[hh] = total.astype(BF)
        if step == 2:
            for copy in d_z.first:
                go(copy)
        elif step:
            go(d_z.direct[step // 2])
    d_z.pass_on(go)

    def p_x(d, yy):
        return remote(
            sx.at[(x + d) % 4, yy], rx.at[d - 1, yy], pxs.at[d - 1, yy], pxr.at[d - 1, yy], to["x"](d)
        )

    def fold_core(yy):
        for hh in range(4):
            p_c(yy, hh).wait_recv()
            row = pl.multiple_of(((yy * 4 + hh) * 2 + c) * SHARD, 64)
            for q in range(4):
                sx[q, yy, hh] = (
                    pw[pl.ds(row + q * PIECE, PIECE), :].astype(F32)
                    + wc[yy, hh, q * PIECE : (q + 1) * PIECE, :].astype(F32)
                ).astype(BF)
        for d in (2, 1, 3):
            go(p_x(d, yy))

    def p_y(yy):
        d = (yy + 3 - y) % 4
        return remote(ty.at[yy], wy.at[d], pys.at[yy], pyr.at[d], (l * 4 + x, yy * 8 + h * 2 + c))

    def fold_x(yy):
        total = sx[x, yy].astype(F32)
        for d in (1, 3, 2):
            p_x(d, yy).wait_recv()
            total = total + rx[d - 1, yy].astype(F32)
        ty[yy] = total.astype(BF)

        @pl.when(y != yy)
        def _():
            p_y(yy).start()

    p_z = RingSum(tz, wf, wz, (slice(0, 48), slice(48, 80)), pzs, pzr)
    p_l = [
        remote(lb.at[l], lb.at[l], pls.at[d - 1], plr.at[d - 1], to["l"](d)) for d in (1, 2, 3)
    ]
    p_g = [
        remote(og.at[x], og.at[x], pgs.at[d - 1], pgr.at[d - 1], to["x"](d)) for d in (1, 2, 3)
    ]

    def finish():
        total = ty[y].astype(F32)
        for d in (1, 3, 2):
            remote(ty.at[0], wy.at[d - 1], pys.at[0], pyr.at[d - 1], to["y"](1)).wait_recv()
            total = total + wy[d - 1].astype(F32)
        tz[...] = total.astype(BF)
        for copy in p_z.first + p_z.direct:
            go(copy)
        p_z.pass_on(go)
        lb[l] = p_z.result().astype(BF)
        for d in (2, 1, 3):
            go(p_l[d - 1])
        for copy in p_l:
            copy.wait_recv()
        og[x] = (
            (lb[0].astype(F32) + lb[1].astype(F32)) + (lb[2].astype(F32) + lb[3].astype(F32))
        ).astype(BF)
        for d in (2, 1, 3):
            go(p_g[d - 1])

    for yy in (0, 1, 2):
        fold_core(yy)
    total = d_z.result()
    up = total[0:128]
    raw = proj_ref[QPG].astype(F32)
    rk = rsqrt_mean(raw)
    grad_key = (
        rk * up - raw * (rk * rk * rk) * jnp.mean(up * raw, axis=-1, keepdims=True)
    ).astype(BF)
    grad_value = total[128:256].astype(BF)
    gpkv_ref[0] = grad_key
    gpkv_ref[1] = grad_value
    partial(QPG, grad_key)
    partial(QPG + 1, grad_value)
    for hh in range(4):
        go(p_c(3, hh))
    for yy in (0, 1, 2):
        fold_x(yy)
    fold_core(3)
    fold_x(3)
    finish()
    for copy in p_g:
        copy.wait_recv()
    for q in range(4):
        gw_ref[q * PIECE : (q + 1) * PIECE, :] = og[q].astype(F32)
    for copy in sent:
        copy.wait_send()
    for yy in range(4):

        @pl.when(y != yy)
        def _():
            p_y(yy).wait_send()


def tokens_kernel(gpq_ref, gpkv_ref, w_ref, rows_ref, out_ref, acc):
    rows = NBR * BLK
    for col in range(NCB):
        grad = gpq_ref[col] if col < QPG else gpkv_ref[col - QPG]
        spread = lax.dot_general(
            grad,
            w_ref[col * rows : (col + 1) * rows, :],
            (((1,), (1,)), ((), ())),
            preferred_element_type=F32,
        )
        for r in range(NBR):
            at = pl.ds(pl.multiple_of(rows_ref[r, col] * BLK, BLK), BLK)
            piece = spread[:, r * BLK : (r + 1) * BLK]
            if col < NRB // NBR:
                acc[:, at] = piece
            else:
                acc[:, at] += piece
    out_ref[...] = acc[...].astype(BF)


VM = pl.BlockSpec(memory_space=pltpu.VMEM)
SM = pl.BlockSpec(memory_space=pltpu.SMEM)
HB = pl.BlockSpec(memory_space=pl.ANY)
LIMIT = 60 * 1024 * 1024


def dma(*shape):
    return pltpu.SemaphoreType.DMA(shape)


def shape(dims, kind=BF):
    return jax.ShapeDtypeStruct(dims, kind)


def run_forward(tokens, w, block_rows):
    return pl.pallas_call(
        forward_kernel,
        out_shape=(
            shape((2, 4, 4, 256, HD)),
            shape((NCB * NBR * BLK, BLK)),
            shape((NCB, 128, HD)),
            shape((NRB, BLK, 128)),
        ),
        in_specs=[VM, VM, HB],
        out_specs=(HB, HB, VM, VM),
        scratch_shapes=[
            pltpu.SMEM((NBR, NCB), jnp.int32),
            pltpu.VMEM((NRB, 128, BLK), BF),
            pltpu.VMEM((2, 4, 4, 4, PIECE, BLK), BF),
            pltpu.VMEM((NCB * NBR * BLK, BLK), BF),
            pltpu.VMEM((2, 4, 4, 256, HD), BF),
            dma(3), dma(2, 4),
            dma(6), dma(6), dma(3), dma(3), dma(3, 4), dma(3, 4), dma(4, 4), dma(4, 4),
            dma(6), dma(6), dma(3, 4), dma(3, 4), dma(4, 4), dma(4, 4),
        ],
        compiler_params=pltpu.CompilerParams(
            collective_id=0, has_side_effects=True, vmem_limit_bytes=LIMIT
        ),
        name="forward",
    )(tokens, w, block_rows)


def run_attention(pairs, kv, proj, upstream):
    rows = QPG * SPAN
    return pl.pallas_call(
        attention_kernel,
        out_shape=(shape((QPG, 128, HD)), shape((32, 256, HD))),
        in_specs=[HB, HB, VM, VM],
        out_specs=(VM, VM),
        scratch_shapes=[
            pltpu.SMEM((2, 32), jnp.int32),
            dma(3),
            pltpu.VMEM((4096, HD), BF),
            pltpu.VMEM((4096, HD), BF),
            pltpu.VMEM((4096 // CHUNK, HD, CHUNK), BF),
            pltpu.VMEM((4096 // CHUNK, HD, CHUNK), BF),
            pltpu.VMEM((6144 // CHUNK, CHUNK, rows), BF),
            pltpu.VMEM((4096, HD), F32),
            pltpu.VMEM((4096, HD), F32),
            pltpu.VMEM((2, rows, HD), BF),
            pltpu.VMEM((2, HD, rows), BF),
            pltpu.VMEM((2, rows, HD), BF),
            pltpu.VMEM((2, HD, rows), BF),
            pltpu.VMEM((2, 8, rows), F32),
            pltpu.VMEM((HD, rows), F32),
            pltpu.VMEM((8, rows), F32),
        ],
        compiler_params=pltpu.CompilerParams(vmem_limit_bytes=LIMIT),
        name="attention",
    )(pairs, kv, proj, upstream)


def run_reduce(dkv, gpq, proj, tokt, block_rows):
    return pl.pallas_call(
        reduce_kernel,
        out_shape=(shape((SHARD, BLK), F32), shape((2, 128, HD))),
        in_specs=[HB, VM, VM, HB, HB],
        out_specs=(VM, VM),
        scratch_shapes=[
            pltpu.SMEM((NBR, NCB), jnp.int32),
            pltpu.VMEM((NRB, BLK, 128), BF),
            pltpu.VMEM((4, 4, 256, HD), BF),
            dma(6),
            pltpu.VMEM((4, 4, 256, HD), BF),
            pltpu.VMEM((4, 4, 256, HD), BF),
            pltpu.VMEM((3, 4, 256, HD), BF),
            pltpu.VMEM((4, 256, HD), BF),
            pltpu.VMEM((256, HD), BF),
            pltpu.VMEM((2, 256, HD), BF),
            pltpu.VMEM((NCB * NBR * BLK, BLK), BF),
            pltpu.VMEM((4, 4, SHARD, BLK), BF),
            pltpu.VMEM((4, 4, 4, PIECE, BLK), BF),
            pltpu.VMEM((3, 4, 4, PIECE, BLK), BF),
            pltpu.VMEM((4, 4, PIECE, BLK), BF),
            pltpu.VMEM((3, 4, PIECE, BLK), BF),
            pltpu.VMEM((4, PIECE, BLK), BF),
            pltpu.VMEM((PIECE, BLK), BF),
            pltpu.VMEM((2, PIECE, BLK), BF),
            pltpu.VMEM((4, PIECE, BLK), BF),
            pltpu.VMEM((4, PIECE, BLK), BF),
            dma(4), dma(4), dma(3, 4), dma(3, 4), dma(6), dma(6),
            dma(4, 4), dma(4, 4), dma(3, 4), dma(3, 4), dma(4), dma(3),
            dma(6), dma(6), dma(3), dma(3), dma(3), dma(3),
        ],
        compiler_params=pltpu.CompilerParams(
            collective_id=1, has_side_effects=True, vmem_limit_bytes=LIMIT
        ),
        name="reduce",
    )(dkv, gpq, proj, tokt, block_rows)


def run_tokens(gpq, gpkv, w_all, block_rows):
    return pl.pallas_call(
        tokens_kernel,
        out_shape=shape((128, D)),
        in_specs=[VM, VM, VM, SM],
        out_specs=VM,
        scratch_shapes=[pltpu.VMEM((128, D), F32)],
        compiler_params=pltpu.CompilerParams(vmem_limit_bytes=LIMIT),
        name="tokens",
    )(gpq, gpkv, w_all, block_rows)


def per_device(tokens, grad_attn, w_packed, block_rows, span_pairs):
    block_rows, span_pairs = block_rows.T, span_pairs.T
    kv, w_all, proj, tokt = run_forward(tokens[0], w_packed, block_rows)
    gpq, dkv = run_attention(span_pairs, kv.reshape(32, 256, HD), proj, grad_attn[0])
    grad_weights, gpkv = run_reduce(dkv.reshape(2, 4, 4, 256, HD), gpq, proj, tokt, block_rows)
    grad_tokens = run_tokens(gpq, gpkv, w_all, block_rows)
    return (grad_tokens[None], grad_weights)


def solution(mesh):
    in_specs = (P("dp", "ctx", None), P("dp", "ctx", None), P("ctx", None), P(), P())
    out_specs = (P("dp", "ctx", None), P("ctx", None))
    return jax.shard_map(
        per_device, mesh=mesh, in_specs=in_specs, out_specs=out_specs, check_vma=False
    )
```

```python
import functools
import math

import jax
import jax.numpy as jnp
from jax import lax
from jax.experimental import pallas as pl
from jax.experimental.pallas import tpu as pltpu
from jax.sharding import PartitionSpec as P

D = 4096
HD = 128
BLK = 128
QPG = 8
SPAN = 64
NRB = 32
NBR = 8
NCB = 10
EPSILON = 1e-06
SCALE = 1.0 / math.sqrt(HD)
SHARD = 320
PIECE = 80
CHUNK = 512
BF = jnp.bfloat16
F32 = jnp.float32
MESH = pl.DeviceIdType.MESH


def place():
    dp = lax.axis_index("dp")
    ctx = lax.axis_index("ctx")
    return dp % 4, dp // 4, ctx // 8, (ctx // 2) % 4, ctx % 2


def peers():
    x, l, y, h, c = place()

    def at(px, plo, py, ph, pc):
        return (plo * 4 + px, py * 8 + ph * 2 + pc)

    return {
        "x": lambda d: at((x + d) % 4, l, y, h, c),
        "l": lambda d: at(x, (l + d) % 4, y, h, c),
        "y": lambda d: at(x, l, (y + d) % 4, h, c),
        "h": lambda d: at(x, l, y, (h + d) % 4, c),
        "c": lambda d: at(x, l, y, h, (c + d) % 2),
    }


def remote(src, dst, send, recv, device):
    return pltpu.make_async_remote_copy(
        src_ref=src, dst_ref=dst, send_sem=send, recv_sem=recv, device_id=device, device_id_type=MESH
    )


def enter(targets):
    barrier = pltpu.get_barrier_semaphore()
    for target in targets:
        pl.semaphore_signal(barrier, inc=1, device_id=target, device_id_type=MESH)
    pl.semaphore_wait(barrier, len(targets))


class Ring:
    def __init__(self, own, at, send, recv):
        to = peers()
        h = place()[3]
        up, down = to["h"](1), to["h"](3)
        self.own = [
            remote(own(0), at(h, 0), send.at[0], recv.at[0], up),
            remote(own(1), at(h, 1), send.at[1], recv.at[1], down),
            remote(own(1), at(h, 1), send.at[2], recv.at[2], up),
            remote(own(0), at(h, 0), send.at[3], recv.at[3], down),
        ]
        before, after = at((h + 3) % 4, 0), at((h + 1) % 4, 1)
        self.relay = [
            remote(before, before, send.at[4], recv.at[4], up),
            remote(after, after, send.at[5], recv.at[5], down),
        ]


class RingSum:
    def __init__(self, terms, relayed, landed, halves, send, recv):
        to = peers()
        self.h = place()[3]
        up, down = to["h"](1), to["h"](3)
        self.terms, self.relayed, self.landed, self.halves = terms, relayed, landed, halves
        h, (a, b) = self.h, halves
        far, nxt, prev = (h + 2) % 4, (h + 1) % 4, (h + 3) % 4
        self.first = [
            remote(terms.at[far, a], relayed.at[a], send.at[0], recv.at[0], up),
            remote(terms.at[far, b], relayed.at[b], send.at[1], recv.at[1], down),
        ]
        self.direct = [
            remote(terms.at[nxt, b], landed.at[0, b], send.at[2], recv.at[2], up),
            remote(terms.at[prev, a], landed.at[1, a], send.at[3], recv.at[3], down),
        ]
        self.added = [
            remote(terms.at[nxt, a], landed.at[0, a], send.at[4], recv.at[4], up),
            remote(terms.at[prev, b], landed.at[1, b], send.at[5], recv.at[5], down),
        ]

    def pass_on(self, go):
        h, (a, b) = self.h, self.halves
        for index, half, target in ((0, a, (h + 1) % 4), (1, b, (h + 3) % 4)):
            self.first[index].wait_recv()
            self.terms[target, half] = (
                self.terms[target, half].astype(F32) + self.relayed[half].astype(F32)
            ).astype(BF)
            go(self.added[index])

    def result(self):
        for copy in self.direct + self.added:
            copy.wait_recv()
        return (
            self.terms[self.h].astype(F32)
            + self.landed[0].astype(F32)
            + self.landed[1].astype(F32)
        )


def rsqrt_mean(values):
    return lax.rsqrt(jnp.mean(values * values, axis=-1, keepdims=True) + EPSILON)


def forward_kernel(
    tok_ref, w_ref, table_ref, kv_out, w_out, proj_ref, tokt_out,
    rows_ref, tokb, turned, wb, wall, kvb, loc, outs,
    wzs, wzr, wys, wyr, wxs, wxr, wcs, wcr, uys, uyr, uxs, uxr, ucs, ucr, kzs, kzr, kys, kyr, kcs, kcr,
):
    x, l, y, h, c = place()
    to = peers()
    table = pltpu.make_async_copy(table_ref, rows_ref, loc.at[2])
    table.start()
    for b in range(NRB):
        pltpu.make_async_copy(
            tok_ref.at[:, b * BLK : (b + 1) * BLK], tokb.at[b], loc.at[3]
        ).start()
    enter(
        [to[a](d) for a in ("y", "x") for d in (1, 2, 3)] + [to["h"](1), to["h"](3), to["c"](1)]
    )
    sent = []

    def go(copy):
        copy.start()
        sent.append(copy)

    def w_x(d, yy):
        return remote(
            wb.at[c, x, yy], wb.at[c, x, yy], wxs.at[d - 1, yy], wxr.at[d - 1, yy], to["x"](d)
        )

    def w_c(xx, yy):
        piece = wb.at[c, xx, yy]
        return remote(piece, piece, wcs.at[xx, yy], wcr.at[xx, yy], to["c"](1))

    row = pl.multiple_of(x * PIECE, 16)
    mine = pltpu.make_async_copy(w_ref.at[pl.ds(row, PIECE)], wb.at[c, x, y, h], loc.at[0])
    mine.start()
    w_cut = ((0, 48), (48, 32))
    wz = Ring(
        lambda half: w_ref.at[pl.ds(row + w_cut[half][0], w_cut[half][1])],
        lambda hh, half: wb.at[c, x, y, hh, pl.ds(*w_cut[half])],
        wzs,
        wzr,
    )
    for copy in wz.own:
        go(copy)
    pltpu.make_async_copy(tokb, tokb, loc.at[3]).wait()
    for b in range(NRB):
        turned[b] = tokb[b].T
    def u_y(d, hh):
        piece = wb.at[c, x, 3, hh]
        return remote(piece, piece, uys.at[d - 1, hh], uyr.at[d - 1, hh], to["y"](d))

    def u_x(d, hh):
        piece = wb.at[c, x, 3, hh]
        return remote(piece, piece, uxs.at[d - 1, hh], uxr.at[d - 1, hh], to["x"](d))

    def u_c(xx, hh):
        piece = wb.at[c, xx, 3, hh]
        return remote(piece, piece, ucs.at[xx, hh], ucr.at[xx, hh], to["c"](1))

    for step in (0, 1, 3, 2):
        hh = (h + 4 - step) % 4
        if step == 0:
            mine.wait()
        elif step == 1:
            for index in range(2):
                wz.own[index].wait_recv()
                go(wz.relay[index])
            wz.own[2].wait_recv()
        elif step == 3:
            wz.own[3].wait_recv()
        else:
            for copy in wz.relay:
                copy.wait_recv()

        @pl.when(y == 3)
        def _():
            for d in (2, 1, 3):
                u_y(d, hh).start()

        @pl.when(y != 3)
        def _():
            remote(
                wb.at[c, x, 3, hh], wb.at[c, x, 3, hh], uys.at[y, hh], uyr.at[y, hh], to["y"](1)
            ).wait_recv()

        for d in (2, 1, 3):
            go(u_x(d, hh))
        go(u_c(x, hh))

    ys = [
        remote(wb.at[c, x, y], wb.at[c, x, y], wys.at[d - 1], wyr.at[d - 1], to["y"](d))
        for d in (2, 1, 3)
    ]

    @pl.when(y != 3)
    def _():
        for copy in ys:
            copy.start()

    def take_y(yy):
        @pl.when(y != yy)
        def _():
            back = (y + 3 - yy) % 4
            remote(
                wb.at[c, x, yy], wb.at[c, x, yy], wys.at[back], wyr.at[back], to["y"](1)
            ).wait_recv()

        for d in (2, 1, 3):
            go(w_x(d, yy))
        go(w_c(x, yy))

    def forward_x(yy):
        for d in (1, 3, 2):
            w_x(d, yy).wait_recv()
            go(w_c((x + 4 - d) % 4, yy))

    def assemble(yy):
        for xx in range(4):
            if yy == 3:
                for hh in range(4):
                    u_c(xx, hh).wait_recv()
            else:
                w_c(xx, yy).wait_recv()
        for cc in range(2):
            for hh in range(4):
                for q in range(4):
                    row = ((yy * 4 + hh) * 2 + cc) * SHARD + q * PIECE
                    wall[row : row + PIECE, :] = wb[cc, q, yy, hh]

    def project(col):
        chosen = jnp.concatenate(
            [tokb[rows_ref[r, col]] for r in range(NBR)], axis=1
        )
        rows = NBR * BLK
        return jnp.dot(
            chosen, wall[col * rows : (col + 1) * rows, :], preferred_element_type=F32
        ).astype(BF)

    save_t = pltpu.make_async_copy(turned, tokt_out, loc.at[4])
    save_t.start()
    for step in (0, 1, 3, 2):
        hh = (h + 4 - step) % 4
        for d in (1, 3, 2):
            u_x(d, hh).wait_recv()
            go(u_c((x + 4 - d) % 4, hh))
    table.wait()
    assemble(3)
    key = project(QPG)
    value = project(QPG + 1)
    proj_ref[QPG] = key
    proj_ref[QPG + 1] = value
    wide = key.astype(F32)
    kvb[c, y, h, 0:128, :] = (wide * rsqrt_mean(wide)).astype(BF)
    kvb[c, y, h, 128:256, :] = value

    def k_y(d, hh):
        piece = kvb.at[c, y, hh]
        return remote(piece, piece, kys.at[d - 1, hh], kyr.at[d - 1, hh], to["y"](d))

    def k_c(yy, hh):
        piece = kvb.at[c, yy, hh]
        return remote(piece, piece, kcs.at[yy, hh], kcr.at[yy, hh], to["c"](1))

    k_cut = ((0, 128), (128, 128))
    kz = Ring(
        lambda half: kvb.at[c, y, h, pl.ds(*k_cut[half])],
        lambda hh, half: kvb.at[c, y, hh, pl.ds(*k_cut[half])],
        kzs,
        kzr,
    )
    for copy in kz.own:
        go(copy)
    for d in (2, 1, 3):
        go(k_y(d, h))
    go(k_c(y, h))
    for yy in (0, 1, 2):
        take_y(yy)
    for index in range(2):
        kz.own[index].wait_recv()
        go(kz.relay[index])
    for d in (1, 3, 2):
        for copy in {1: (kz.own[2],), 3: (kz.own[3],), 2: kz.relay}[d]:
            copy.wait_recv()
        hh = (h + 4 - d) % 4
        for e in (2, 1, 3):
            go(k_y(e, hh))
        go(k_c(y, hh))
    for yy in (0, 1, 2):
        forward_x(yy)

    def forward_k(step):
        hh = (h + 4 - step) % 4
        for d in (1, 3, 2):
            k_y(d, hh).wait_recv()
            go(k_c((y + 4 - d) % 4, hh))

    for step in (0, 1, 3):
        forward_k(step)
    for yy in (0, 1, 2):
        assemble(yy)
    save_w = pltpu.make_async_copy(wall, w_out, loc.at[1])
    save_w.start()
    for col in range(QPG):
        proj_ref[col] = project(col)
    forward_k(2)
    saves = []
    for step in (0, 1, 3, 2):
        hh = (h + 4 - step) % 4
        for yy in range(4):
            k_c(yy, hh).wait_recv()
        for cc in range(2):
            save = pltpu.make_async_copy(kvb.at[cc, :, hh], kv_out.at[cc, :, hh], outs.at[cc, step])
            save.start()
            saves.append(save)
    for copy in sent:
        copy.wait_send()

    @pl.when(y != 3)
    def _():
        for copy in ys:
            copy.wait_send()

    @pl.when(y == 3)
    def _():
        for hh in range(4):
            for d in (1, 2, 3):
                u_y(d, hh).wait_send()

    for save in saves:
        save.wait()
    save_w.wait()
    save_t.wait()


def attention_kernel(
    table_ref, kv_ref, proj_ref, up_ref, gp_ref, dkv_ref,
    pairs_ref, sems, ks, vs, kt, vt, es, dk, dv, qh, qt, gg, gt, dd, acc, tot,
):
    me = lax.axis_index("ctx")

    table = pltpu.make_async_copy(table_ref, pairs_ref, sems.at[0])
    table.start()

    def gather(owner, _):
        spot = (owner % 2) * 16 + owner // 2
        for part in range(2):
            at = pl.ds(pl.multiple_of(pairs_ref[part, owner] * SPAN, SPAN), SPAN)
            for half, into in ((0, ks), (1, vs)):
                pltpu.make_async_copy(
                    kv_ref.at[spot, pl.ds(half * 128 + part * SPAN, SPAN)],
                    into.at[at],
                    sems.at[1 + half],
                ).start()
        return 0

    def chunks(part):
        return ((pairs_ref[part, me] + 1) * SPAN + CHUNK - 1) // CHUNK

    def rows_of(index):
        return pl.ds(pl.multiple_of(index * CHUNK, CHUNK), CHUNK)

    def flip(index, _):
        kt[index] = ks[rows_of(index), :].T
        vt[index] = vs[rows_of(index), :].T
        return 0

    def part_rows(part, head):
        return slice(head * SPAN, (head + 1) * SPAN), slice(part * SPAN, (part + 1) * SPAN)

    table.wait()
    lax.fori_loop(0, 32, gather, 0)
    for part in range(2):
        for head in range(QPG):
            put, get = part_rows(part, head)
            raw = proj_ref[head, get, :].astype(F32)
            qh[part, put, :] = (raw * rsqrt_mean(raw)).astype(BF)
            gg[part, put, :] = up_ref[get, head * HD : (head + 1) * HD]
        qt[part] = qh[part].T

    pltpu.make_async_copy(ks, ks, sems.at[1]).wait()
    pltpu.make_async_copy(vs, vs, sems.at[2]).wait()
    lax.fori_loop(0, chunks(1), flip, 0)
    factor = SCALE * math.log2(math.e)

    def forward(part):
        count = chunks(part)
        acc[...] = jnp.zeros_like(acc)
        tot[...] = jnp.zeros_like(tot)

        def tile(index, masked):
            score = jnp.dot(ks[rows_of(index), :], qt[part], preferred_element_type=F32)
            expo = jnp.exp2(score * factor)
            if masked:
                key_pos = index * CHUNK + lax.broadcasted_iota(jnp.int32, expo.shape, 0)
                query_pos = pairs_ref[part, me] * SPAN + lax.broadcasted_iota(
                    jnp.int32, expo.shape, 1
                ) % SPAN
                expo = jnp.where(key_pos <= query_pos, expo, 0.0)
            tot[...] += jnp.sum(expo.reshape(CHUNK // 8, 8, expo.shape[1]), axis=0)
            low = expo.astype(BF)
            es[part * (2048 // CHUNK) + index] = low
            acc[...] += jnp.dot(vt[index], low, preferred_element_type=F32)

        def step(index, _):
            tile(index, False)
            return 0

        lax.fori_loop(0, count - 1, step, 0)
        tile(count - 1, True)
        inverse = 1.0 / jnp.sum(tot[...], axis=0, keepdims=True)
        up = gg[part].astype(F32).T
        delta = jnp.sum(up * (acc[...] * inverse), axis=0, keepdims=True)
        scaled = inverse * SCALE
        low = (up * scaled).astype(BF)
        gt[part] = low
        gg[part] = low.T
        dd[part] = jnp.broadcast_to(delta * scaled, dd.shape[1:])

    def backward(part, first):
        count = chunks(part)
        acc[...] = jnp.zeros_like(acc)

        def step(index, _):
            low = es[part * (2048 // CHUNK) + index]
            dprob = jnp.dot(vs[rows_of(index), :], gt[part], preferred_element_type=F32)
            dscore = (low.astype(F32) * (dprob - dd[part, 0:1, :])).astype(BF)
            more_k = jnp.dot(dscore, qh[part], preferred_element_type=F32)
            more_v = jnp.dot(low, gg[part], preferred_element_type=F32)
            if first:
                dk[rows_of(index), :] = more_k
                dv[rows_of(index), :] = more_v
            else:
                dk[rows_of(index), :] += more_k
                dv[rows_of(index), :] += more_v
            acc[...] += jnp.dot(kt[index], dscore, preferred_element_type=F32)
            return 0

        lax.fori_loop(0, count, step, 0)
        grad = acc[...].T
        for head in range(QPG):
            put, get = part_rows(part, head)
            up = grad[put, :]
            raw = proj_ref[head, get, :].astype(F32)
            rq = rsqrt_mean(raw)
            gp_ref[head, get, :] = (
                rq * up - raw * (rq * rq * rq) * jnp.mean(up * raw, axis=-1, keepdims=True)
            ).astype(BF)

    forward(1)
    forward(0)
    backward(1, True)
    backward(0, False)

    def clear(index, _):
        dk[rows_of(index), :] = jnp.zeros((CHUNK, HD), F32)
        dv[rows_of(index), :] = jnp.zeros((CHUNK, HD), F32)
        return 0

    lax.fori_loop(chunks(1), 4096 // CHUNK, clear, 0)

    def scatter(block, _):
        for step in range(4):
            owner = block * 4 + step
            spot = (step % 2) * 16 + block * 2 + step // 2
            for part in range(2):
                at = pl.ds(pl.multiple_of(pairs_ref[part, owner] * SPAN, SPAN), SPAN)
                low = part * SPAN
                dkv_ref[spot, low : low + SPAN, :] = dk[at, :].astype(BF)
                dkv_ref[spot, 128 + low : 128 + low + SPAN, :] = (
                    dv[at, :] * math.sqrt(HD)
                ).astype(BF)
        return 0

    lax.fori_loop(0, 8, scatter, 0)


def reduce_kernel(
    dkv_ref, gpq_ref, proj_ref, tokens_ref, table_ref, gw_ref, gpkv_ref,
    rows_ref, tokt_ref, dl, loc, rc, sb, ry, s2, rf, rz, pw, wc, sx, rx, ty, wy, tz, wf, wz, lb, og,
    dcs, dcr, dys, dyr, dzs, dzr, pcs, pcr, pxs, pxr, pys, pyr, vxs, vxr, vys, vyr, pzs, pzr, pls, plr, pgs, pgr,
):
    x, l, y, h, c = place()
    to = peers()
    table = pltpu.make_async_copy(table_ref, rows_ref, loc.at[4])
    turned = pltpu.make_async_copy(tokens_ref, tokt_ref, loc.at[5])
    loads = [
        pltpu.make_async_copy(dkv_ref.at[c, :, hh], dl.at[:, hh], loc.at[hh]) for hh in range(4)
    ]
    for copy in loads + [table, turned]:
        copy.start()
    enter(
        [to[a](d) for a in ("y", "x", "l") for d in (1, 2, 3)]
        + [to["h"](1), to["h"](3), to["c"](1)]
    )
    sent = []

    def go(copy):
        copy.start()
        sent.append(copy)

    def d_c(hh):
        return remote(
            dkv_ref.at[1 - c, :, hh], rc.at[:, hh], dcs.at[hh], dcr.at[hh], to["c"](1)
        )

    for step in (2, 1, 3, 0):
        go(d_c((h + step) % 4))

    def partial(col, grad):
        chosen = jnp.concatenate([tokt_ref[rows_ref[r, col]] for r in range(NBR)], axis=0)
        rows = NBR * BLK
        pw[col * rows : (col + 1) * rows, :] = jnp.dot(
            chosen, grad, preferred_element_type=F32
        ).astype(BF)

    def d_y(d, hh):
        return remote(
            sb.at[(y + d) % 4, hh], ry.at[d - 1, hh], dys.at[d - 1, hh], dyr.at[d - 1, hh], to["y"](d)
        )

    for copy in loads:
        copy.wait()
    for step in (2, 1, 3, 0):
        hh = (h + step) % 4
        d_c(hh).wait_recv()
        for d in (2, 1, 3, 0):
            yy = (y + d) % 4
            sb[yy, hh] = (dl[yy, hh].astype(F32) + rc[yy, hh].astype(F32)).astype(BF)
            if d:
                go(d_y(d, hh))

    def p_c(yy, hh):
        row = ((yy * 4 + hh) * 2 + 1 - c) * SHARD
        return remote(
            pw.at[pl.ds(pl.multiple_of(row, 64), SHARD)],
            wc.at[yy, hh],
            pcs.at[yy, hh],
            pcr.at[yy, hh],
            to["c"](1),
        )

    table.wait()
    turned.wait()
    for col in range(QPG):
        partial(col, gpq_ref[col])
    for yy in (0, 1, 2):
        for hh in range(4):
            go(p_c(yy, hh))

    d_z = RingSum(s2, rf, rz, (slice(0, 128), slice(128, 256)), dzs, dzr)
    for step in (2, 1, 3, 0):
        hh = (h + step) % 4
        total = sb[y, hh].astype(F32)
        for d in (1, 3, 2):
            d_y(d, hh).wait_recv()
            total = total + ry[d - 1, hh].astype(F32)
        s2[hh] = total.astype(BF)
        if step == 2:
            for copy in d_z.first:
                go(copy)
        elif step:
            go(d_z.direct[step // 2])

    def p_x(d, yy):
        return remote(
            sx.at[(x + d) % 4, yy], rx.at[d - 1, yy], pxs.at[d - 1, yy], pxr.at[d - 1, yy], to["x"](d)
        )

    def fold_piece(yy, hh):
        p_c(yy, hh).wait_recv()
        row = pl.multiple_of(((yy * 4 + hh) * 2 + c) * SHARD, 64)
        for q in range(4):
            sx[q, yy, hh] = (
                pw[pl.ds(row + q * PIECE, PIECE), :].astype(F32)
                + wc[yy, hh, q * PIECE : (q + 1) * PIECE, :].astype(F32)
            ).astype(BF)

    def fold_core(yy):
        for hh in range(4):
            fold_piece(yy, hh)
        for d in (2, 1, 3):
            go(p_x(d, yy))

    def v_x(d, hh):
        return remote(
            sx.at[(x + d) % 4, 3, hh],
            rx.at[d - 1, 3, hh],
            vxs.at[d - 1, hh],
            vxr.at[d - 1, hh],
            to["x"](d),
        )

    def v_y(hh):
        d = (2 - y) % 4
        return remote(
            ty.at[3, hh], wy.at[d, hh], vys.at[hh], vyr.at[d, hh], (l * 4 + x, 24 + h * 2 + c)
        )

    order = [(h + step) % 4 for step in (2, 1, 3, 0)]

    def p_y(yy):
        d = (yy + 3 - y) % 4
        return remote(ty.at[yy], wy.at[d], pys.at[yy], pyr.at[d], (l * 4 + x, yy * 8 + h * 2 + c))

    def fold_x(yy):
        total = sx[x, yy].astype(F32)
        for d in (1, 3, 2):
            p_x(d, yy).wait_recv()
            total = total + rx[d - 1, yy].astype(F32)
        ty[yy] = total.astype(BF)

        @pl.when(y != yy)
        def _():
            p_y(yy).start()

    p_z = RingSum(tz, wf, wz, (slice(0, 48), slice(48, 80)), pzs, pzr)
    p_l = [
        remote(lb.at[l], lb.at[l], pls.at[d - 1], plr.at[d - 1], to["l"](d)) for d in (1, 2, 3)
    ]
    p_g = [
        remote(og.at[x], og.at[x], pgs.at[d - 1], pgr.at[d - 1], to["x"](d)) for d in (1, 2, 3)
    ]

    def finish():
        starts = p_z.first + p_z.direct

        @pl.when(y != 3)
        def _():
            total = ty[y].astype(F32)
            for d in (1, 3, 2):
                remote(ty.at[0], wy.at[d - 1], pys.at[0], pyr.at[d - 1], to["y"](1)).wait_recv()
                total = total + wy[d - 1].astype(F32)
            tz[...] = total.astype(BF)
            for copy in starts:
                copy.start()

        @pl.when(y == 3)
        def _():
            for index, hh in enumerate(order):
                total = ty[3, hh].astype(F32)
                for d in (1, 3, 2):
                    remote(
                        ty.at[0, 0], wy.at[d - 1, hh], vys.at[0], vyr.at[d - 1, hh], to["y"](1)
                    ).wait_recv()
                    total = total + wy[d - 1, hh].astype(F32)
                tz[hh] = total.astype(BF)
                for copy in (starts[:2], starts[2:3], starts[3:], [])[index]:
                    copy.start()

        sent.extend(starts)
        p_z.pass_on(go)
        lb[l] = p_z.result().astype(BF)
        for d in (2, 1, 3):
            go(p_l[d - 1])
        for copy in p_l:
            copy.wait_recv()
        og[x] = (
            (lb[0].astype(F32) + lb[1].astype(F32)) + (lb[2].astype(F32) + lb[3].astype(F32))
        ).astype(BF)
        for d in (2, 1, 3):
            go(p_g[d - 1])

    d_z.pass_on(go)
    for yy in (0, 1, 2):
        fold_core(yy)
    total = d_z.result()
    up = total[0:128]
    raw = proj_ref[QPG].astype(F32)
    rk = rsqrt_mean(raw)
    grad_key = (
        rk * up - raw * (rk * rk * rk) * jnp.mean(up * raw, axis=-1, keepdims=True)
    ).astype(BF)
    grad_value = total[128:256].astype(BF)
    gpkv_ref[0] = grad_key
    gpkv_ref[1] = grad_value
    partial(QPG, grad_key)
    partial(QPG + 1, grad_value)
    for hh in order:
        go(p_c(3, hh))
    for hh in order:
        fold_piece(3, hh)
        for d in (2, 1, 3):
            go(v_x(d, hh))
    for yy in (0, 1, 2):
        fold_x(yy)
    for hh in order:
        total = sx[x, 3, hh].astype(F32)
        for d in (1, 3, 2):
            v_x(d, hh).wait_recv()
            total = total + rx[d - 1, 3, hh].astype(F32)
        ty[3, hh] = total.astype(BF)

        @pl.when(y != 3)
        def _():
            v_y(hh).start()

    finish()
    for copy in p_g:
        copy.wait_recv()
    for q in range(4):
        gw_ref[q * PIECE : (q + 1) * PIECE, :] = og[q]
    for copy in sent:
        copy.wait_send()
    for yy in range(3):

        @pl.when(y != yy)
        def _():
            p_y(yy).wait_send()

    @pl.when(y != 3)
    def _():
        for hh in range(4):
            v_y(hh).wait_send()


def tokens_kernel(gpq_ref, gpkv_ref, w_ref, gw_ref, rows_ref, out_ref, weights_ref, acc):
    weights_ref[...] = gw_ref[...].astype(F32)
    rows = NBR * BLK
    for col in range(NCB):
        grad = gpq_ref[col] if col < QPG else gpkv_ref[col - QPG]
        spread = lax.dot_general(
            grad,
            w_ref[col * rows : (col + 1) * rows, :],
            (((1,), (1,)), ((), ())),
            preferred_element_type=F32,
        )
        for r in range(NBR):
            at = pl.ds(pl.multiple_of(rows_ref[r, col] * BLK, BLK), BLK)
            piece = spread[:, r * BLK : (r + 1) * BLK]
            if col < NRB // NBR:
                acc[:, at] = piece
            else:
                acc[:, at] += piece
    out_ref[...] = acc[...].astype(BF)


VM = pl.BlockSpec(memory_space=pltpu.VMEM)
SM = pl.BlockSpec(memory_space=pltpu.SMEM)
HB = pl.BlockSpec(memory_space=pl.ANY)
LIMIT = 60 * 1024 * 1024


def dma(*shape):
    return pltpu.SemaphoreType.DMA(shape)


def shape(dims, kind=BF):
    return jax.ShapeDtypeStruct(dims, kind)


def run_forward(tokens, w, block_rows):
    return pl.pallas_call(
        forward_kernel,
        out_shape=(
            shape((2, 4, 4, 256, HD)),
            shape((NCB * NBR * BLK, BLK)),
            shape((NCB, 128, HD)),
            shape((NRB, BLK, 128)),
        ),
        in_specs=[HB, VM, HB],
        out_specs=(HB, HB, VM, HB),
        scratch_shapes=[
            pltpu.SMEM((NBR, NCB), jnp.int32),
            pltpu.VMEM((NRB, 128, BLK), BF),
            pltpu.VMEM((NRB, BLK, 128), BF),
            pltpu.VMEM((2, 4, 4, 4, PIECE, BLK), BF),
            pltpu.VMEM((NCB * NBR * BLK, BLK), BF),
            pltpu.VMEM((2, 4, 4, 256, HD), BF),
            dma(5), dma(2, 4),
            dma(6), dma(6), dma(3), dma(3), dma(3, 3), dma(3, 3), dma(4, 3), dma(4, 3),
            dma(3, 4), dma(3, 4), dma(3, 4), dma(3, 4), dma(4, 4), dma(4, 4),
            dma(6), dma(6), dma(3, 4), dma(3, 4), dma(4, 4), dma(4, 4),
        ],
        compiler_params=pltpu.CompilerParams(
            collective_id=0, has_side_effects=True, vmem_limit_bytes=LIMIT
        ),
        name="forward",
    )(tokens, w, block_rows)


def run_attention(pairs, kv, proj, upstream):
    rows = QPG * SPAN
    return pl.pallas_call(
        attention_kernel,
        out_shape=(shape((QPG, 128, HD)), shape((32, 256, HD))),
        in_specs=[HB, HB, VM, VM],
        out_specs=(VM, VM),
        scratch_shapes=[
            pltpu.SMEM((2, 32), jnp.int32),
            dma(3),
            pltpu.VMEM((4096, HD), BF),
            pltpu.VMEM((4096, HD), BF),
            pltpu.VMEM((4096 // CHUNK, HD, CHUNK), BF),
            pltpu.VMEM((4096 // CHUNK, HD, CHUNK), BF),
            pltpu.VMEM((6144 // CHUNK, CHUNK, rows), BF),
            pltpu.VMEM((4096, HD), F32),
            pltpu.VMEM((4096, HD), F32),
            pltpu.VMEM((2, rows, HD), BF),
            pltpu.VMEM((2, HD, rows), BF),
            pltpu.VMEM((2, rows, HD), BF),
            pltpu.VMEM((2, HD, rows), BF),
            pltpu.VMEM((2, 8, rows), F32),
            pltpu.VMEM((HD, rows), F32),
            pltpu.VMEM((8, rows), F32),
        ],
        compiler_params=pltpu.CompilerParams(vmem_limit_bytes=LIMIT),
        name="attention",
    )(pairs, kv, proj, upstream)


def run_reduce(dkv, gpq, proj, tokt, block_rows):
    return pl.pallas_call(
        reduce_kernel,
        out_shape=(shape((SHARD, BLK)), shape((2, 128, HD))),
        in_specs=[HB, VM, VM, HB, HB],
        out_specs=(VM, VM),
        scratch_shapes=[
            pltpu.SMEM((NBR, NCB), jnp.int32),
            pltpu.VMEM((NRB, BLK, 128), BF),
            pltpu.VMEM((4, 4, 256, HD), BF),
            dma(6),
            pltpu.VMEM((4, 4, 256, HD), BF),
            pltpu.VMEM((4, 4, 256, HD), BF),
            pltpu.VMEM((3, 4, 256, HD), BF),
            pltpu.VMEM((4, 256, HD), BF),
            pltpu.VMEM((256, HD), BF),
            pltpu.VMEM((2, 256, HD), BF),
            pltpu.VMEM((NCB * NBR * BLK, BLK), BF),
            pltpu.VMEM((4, 4, SHARD, BLK), BF),
            pltpu.VMEM((4, 4, 4, PIECE, BLK), BF),
            pltpu.VMEM((3, 4, 4, PIECE, BLK), BF),
            pltpu.VMEM((4, 4, PIECE, BLK), BF),
            pltpu.VMEM((3, 4, PIECE, BLK), BF),
            pltpu.VMEM((4, PIECE, BLK), BF),
            pltpu.VMEM((PIECE, BLK), BF),
            pltpu.VMEM((2, PIECE, BLK), BF),
            pltpu.VMEM((4, PIECE, BLK), BF),
            pltpu.VMEM((4, PIECE, BLK), BF),
            dma(4), dma(4), dma(3, 4), dma(3, 4), dma(6), dma(6),
            dma(4, 4), dma(4, 4), dma(3, 3), dma(3, 3), dma(3), dma(3),
            dma(3, 4), dma(3, 4), dma(4), dma(3, 4),
            dma(6), dma(6), dma(3), dma(3), dma(3), dma(3),
        ],
        compiler_params=pltpu.CompilerParams(
            collective_id=1, has_side_effects=True, vmem_limit_bytes=LIMIT
        ),
        name="reduce",
    )(dkv, gpq, proj, tokt, block_rows)


def run_tokens(gpq, gpkv, w_all, sums, block_rows):
    return pl.pallas_call(
        tokens_kernel,
        out_shape=(shape((128, D)), shape((SHARD, BLK), F32)),
        in_specs=[VM, VM, VM, VM, SM],
        out_specs=(VM, VM),
        scratch_shapes=[pltpu.VMEM((128, D), F32)],
        compiler_params=pltpu.CompilerParams(vmem_limit_bytes=LIMIT),
        name="tokens",
    )(gpq, gpkv, w_all, sums, block_rows)


def per_device(tokens, grad_attn, w_packed, block_rows, span_pairs):
    block_rows, span_pairs = block_rows.T, span_pairs.T
    kv, w_all, proj, tokt = run_forward(tokens[0], w_packed, block_rows)
    gpq, dkv = run_attention(span_pairs, kv.reshape(32, 256, HD), proj, grad_attn[0])
    sums, gpkv = run_reduce(dkv.reshape(2, 4, 4, 256, HD), gpq, proj, tokt, block_rows)
    grad_tokens, grad_weights = run_tokens(gpq, gpkv, w_all, sums, block_rows)
    return (grad_tokens[None], grad_weights)


def solution(mesh):
    in_specs = (P("dp", "ctx", None), P("dp", "ctx", None), P("ctx", None), P(), P())
    out_specs = (P("dp", "ctx", None), P("ctx", None))
    return jax.shard_map(
        per_device, mesh=mesh, in_specs=in_specs, out_specs=out_specs, check_vma=False
    )
```
